128 devices in a mesh: req: 16 (over x, y), head: 8 (over z, core).
Axes of the slice: x: 4, y: 4, z: 4, core: 2. Of those that a mesh axis runs over, the one named last changes fastest.
Arguments:
- hidden: bfloat16 [4096, 2048], P('req'), may hold values from -6 to 6
- attn_gain: float32 [2048], replicated, may hold values from 0.1 to 1.9
- attn_router: float32 [2048, 4], replicated, may hold values from -8 to 8
- attention_expert_pairs: int32 [4096, 2], P('req'), may hold values from 0 to 3, all different within a row
- key_value_weight: bfloat16 [2, 2048, 2048], P(None, None, 'head'), may hold values from -0.125 to 0.125
- query_weight: bfloat16 [4, 2048, 2048], P(None, None, 'head'), may hold values from -0.125 to 0.125
- output_weight: bfloat16 [4, 2048, 2048], P(None, 'head'), may hold values from -0.125 to 0.125
- paged_key_value_cache: bfloat16 [2, 512, 128, 2048], P(None, 'req', None, 'head'), may hold values from -70 to 70
- page_table: int32 [64, 30], P('req'), may hold values from 0 to 29, as said below
- cache_len: int32 [64], P('req'), may hold values from 1 to 3312, as said below
- ancestor: int32 [64, 64, 64], P('req'), may hold values from 0 to 1, as said below
- ffn_gain: float32 [2048], replicated, may hold values from 0.1 to 1.9
- ffn_router: float32 [2048, 8], replicated, may hold values from -8 to 8
- ffn_route: int32 [4096, 2], P('req'), may hold values from 0 to 7, all different within a row; in each aligned block of 256 rows (0 to 255, 256 to 511, ...) at most 96 rows name the same one
- w_gate_up: bfloat16 [8, 2, 5632, 2048], P('head', None, 'req'), may hold values from -0.125 to 0.125
- w_down: bfloat16 [8, 5632, 2048], P('head', 'req'), may hold values from -0.078125 to 0.078125
- accept_path: int32 [64, 16], P('req'), may hold values from 0 to 30, as said below
- accept_count: int32 [64], P('req'), may hold values from 1 to 16
- mig_slot: int32 [16], P('req'), may hold values from 0 to 3, as said below
- destination: int32 [16], replicated, may hold values from 0 to 15, as said below
Outputs:
- layer_out: bfloat16 [4096, 2048], P(('req', 'head'))
- kv_out: bfloat16 [2, 512, 128, 2048], P(None, 'req', None, 'head')
The draws below stay inside these ranges and needn't reach their ends.
Inputs may be any that keep to these rules, and one draw needn't show every extreme that they name: `page_table`: with n_i = ceil((cache_len[i] + 16) / 128), entries j < n_i of row i are distinct slots below 30, unlike those of the other requests of the same row of requests, and the n_i of one row sum to exactly 30; later entries are 0 and unused. `cache_len`: one request of each row holds most of the row's pages; the largest value is reached in some row. ancestor[i, a, b] = 1 exactly where b is a or an ancestor of a in request i's tree; a token's parent has a lower index, one or two below its own, and token 0 is the root. For t < accept_count[i], accept_path[i, t] is the token of depth t on one path from the root of request i's tree; later entries are 0. `mig_slot`: the moving request has exactly 2 pages. `destination`: A permutation of the rows in which no row maps to itself. `ffn_route`: in the 256 rows of one index of req no expert is named by more than 96 rows; the entries of a row differ. `attention_expert_pairs`: the entries of a row differ.
All inputs are finite; a program needn't handle non-finite values.
Results may differ from the reference program's by a relative error of at most 0.023.
Values may be sent and summed in bfloat16 or wider, within the bound.
A program may use at most 128 MiB of HBM per device.

```python
import math
import jax
import jax.numpy as jnp
import numpy as np
from jax import lax

MODEL_WIDTH = 2048
KEY_VALUE_HEADS = 16
HEAD_SIZE = 128
ATTN_EXPERTS = 4
TOPK = 2
FEXP = 8
FF = 5632
DRAFT = 64
ACC = 16
PAGE_POSITIONS = 128
MIGP = 2
R_DEV = 4
REQS = 64
ROW_TOK = 256
DRAFT_TOKENS = 4096
PAGES = 32
TABLE_ENTRIES = 30
TOTAL_PAGES = 512
CAP = 96
N_REQ = 16


def cache_layout(key):
    base_key = jax.random.fold_in(key, 11)
    forced_row = jax.random.randint(jax.random.fold_in(base_key, 5), (), 0, N_REQ)

    def one_row(row_key, is_forced):
        sub_keys = jax.random.split(row_key, 5)
        moving = jax.random.randint(sub_keys[0], (), 0, R_DEV)
        moving = jnp.where(is_forced, R_DEV - 1, moving)
        heavy_req = (moving + 1 + jax.random.randint(sub_keys[1], (), 0, R_DEV - 1)) % R_DEV
        others = jax.random.randint(sub_keys[2], (R_DEV,), 1, 5)
        others = jnp.where(is_forced, 1, others)
        req_ids = jnp.arange(R_DEV)
        counts = jnp.where(req_ids == moving, MIGP, others)
        counts = jnp.where(req_ids == heavy_req, 0, counts)
        counts = jnp.where(req_ids == heavy_req, PAGES - MIGP - jnp.sum(counts), counts)
        extra_len = jax.random.randint(sub_keys[3], (R_DEV,), 0, PAGE_POSITIONS)
        extra_len = jnp.where(req_ids == heavy_req, PAGE_POSITIONS - 1, extra_len)
        lengths = jnp.maximum(1, (counts - 1) * PAGE_POSITIONS - ACC + 1 + extra_len)
        slot_order = jax.random.permutation(sub_keys[4], PAGES - MIGP)
        offsets = jnp.cumsum(counts) - counts
        entry_ids = jnp.arange(TABLE_ENTRIES)
        spot_index = jnp.minimum(offsets[:, None] + entry_ids[None, :], PAGES - MIGP - 1)
        page_slots = jnp.where(entry_ids[None, :] < counts[:, None], slot_order[spot_index], 0)
        return (lengths, page_slots, moving)
    forced_flags = jnp.arange(N_REQ) == forced_row
    lengths, page_slots, moving = jax.vmap(one_row)(jax.random.split(base_key, N_REQ), forced_flags)
    return (lengths.reshape(REQS).astype(jnp.int32), page_slots.reshape(REQS, TABLE_ENTRIES).astype(jnp.int32), moving.astype(jnp.int32))


def draw_cache_len(key, part):
    return cache_layout(key)[0]


def draw_page_table(key, part):
    return cache_layout(key)[1]


def draw_mig_slot(key, part):
    return cache_layout(key)[2]


def draw_destination(key, part):
    order_ids = jax.random.permutation(jax.random.fold_in(key, 31), N_REQ)
    return jnp.zeros((N_REQ,), jnp.int32).at[order_ids].set(jnp.roll(order_ids, -1)).astype(jnp.int32)


def tree_layout(key):
    base_key = jax.random.fold_in(key, 23)
    forced = jax.random.randint(jax.random.fold_in(base_key, 7), (), 0, REQS)

    def one_request(req_key, is_forced):
        sub_keys = jax.random.split(req_key, 2)
        node_ids = jnp.arange(DRAFT)
        step_back = jax.random.randint(sub_keys[0], (DRAFT,), 0, 2)
        step_back = jnp.where(is_forced, 1, step_back)
        parents = jnp.maximum(0, node_ids - 1 - step_back)

        def extend(node, tree_mask):
            row_bits = tree_mask[parents[node]].at[node].set(1)
            return tree_mask.at[node].set(row_bits)
        tree_mask = lax.fori_loop(1, DRAFT, extend, jnp.eye(DRAFT, dtype=jnp.int32))
        return (tree_mask, jax.random.randint(sub_keys[1], (), 1, ACC + 1))
    forced_flags = jnp.arange(REQS) == forced
    trees, counts = jax.vmap(one_request)(jax.random.split(base_key, REQS), forced_flags)
    counts = jnp.where(forced_flags, ACC, counts)
    tree_depth = jnp.sum(trees, axis=2) - 1
    at_depth = tree_depth == counts[:, None] - 1
    target = DRAFT - 1 - jnp.argmax(at_depth[:, ::-1], axis=1)
    ancestors_of = trees[jnp.arange(REQS), target]
    step_ids = jnp.arange(ACC)
    on_path = (ancestors_of[:, None, :] > 0) & (tree_depth[:, None, :] == step_ids[None, :, None])
    path_nodes = jnp.argmax(on_path, axis=2)
    path_nodes = jnp.where(step_ids[None, :] < counts[:, None], path_nodes, 0)
    return (trees.astype(jnp.int32), path_nodes.astype(jnp.int32), counts.astype(jnp.int32))


def draw_ancestor(key, part):
    return tree_layout(key)[0]


def draw_accept_path(key, part):
    return tree_layout(key)[1]


def draw_accept_count(key, part):
    return tree_layout(key)[2]


def draw_paged_key_value_cache(key, part):
    tensor_extent = (2, TOTAL_PAGES, PAGE_POSITIONS, KEY_VALUE_HEADS * HEAD_SIZE)
    main_key = jax.random.fold_in(key, 41)
    values = jnp.clip(jax.random.normal(main_key, tensor_extent, jnp.float32), -6.0, 6.0)
    return values.astype(jnp.bfloat16)


def router_draw(key, salt, experts):
    main_key = jax.random.fold_in(key, salt)
    values = jnp.clip(jax.random.normal(main_key, (MODEL_WIDTH, experts), jnp.float32), -5.0, 5.0) * MODEL_WIDTH ** (-0.5)
    return values.astype(jnp.float32)


def draw_attn_router(key, part):
    return router_draw(key, 51, ATTN_EXPERTS)


def draw_ffn_router(key, part):
    return router_draw(key, 53, FEXP)


def steps_of(own_key, shape, pieces, least, largest):
    level = 1.0
    for axis_at, blocks in pieces:
        heights = jax.random.uniform(jax.random.fold_in(jax.random.fold_in(own_key, 6), axis_at), (blocks,), jnp.float32, least / len(pieces), largest / len(pieces))
        level = level * jnp.repeat(jnp.exp(heights), shape[axis_at] // blocks).reshape((-1,) + (1,) * (len(shape) - 1 - axis_at))
    return level


def choose_distinct(key, rows, number_of, top, lift):
    order = jax.random.permutation(jax.random.fold_in(key, 1), number_of)
    favour = order
    for power in range(3):
        favour = favour * favour // number_of
    favour = favour * lift // number_of
    tickets = jax.random.randint(jax.random.fold_in(key, 2), (rows, number_of), 0, 4096) + favour
    sure = jax.random.permutation(jax.random.fold_in(key, 3), rows)[jnp.arange(number_of) % rows]
    tickets = jnp.where(jnp.arange(rows)[:, None] == sure[None, :], 1 << 14, tickets)
    score = tickets * number_of + jnp.arange(number_of)
    return lax.top_k(score.astype(jnp.int32), top)[1].astype(jnp.int32)


def shared_out(rng, own, number, rows, amount, top, reach, lean):
    ranking = jax.random.permutation(rng, amount)
    packed, usual = portions_of(amount, rows * top, reach, lean, True), portions_of(amount, rows * top, reach, lean, False)
    places = jnp.arange(amount)

    def named(tallies, offset_by):
        used = int((tallies > 0).sum())
        fixed = max(1, used // 4)
        passed = fixed + (places - fixed + offset_by * (used - fixed)) % max(1, amount - fixed)
        return jnp.zeros((amount,), jnp.int32).at[ranking[jnp.where(places < fixed, places, passed)]].set(jnp.asarray(tallies, jnp.int32))

    tallies = jnp.where(number % 4 == 0, named(packed, number // 4), named(usual, number - number // 4 - 1))
    mixed = jax.random.permutation(jax.random.fold_in(own, 3), amount)
    donor, sink = mixed[0:amount // 2 * 2:2], mixed[1:amount // 2 * 2:2]
    room = jnp.minimum(tallies[donor] - 1, reach - tallies[sink]) // 2
    room = jnp.where((donor == ranking[0]) | (sink == ranking[0]) | (tallies[sink] == 0), 0, jnp.maximum(room, 0))
    passed = jax.random.randint(jax.random.fold_in(own, 4), (amount // 2,), 0, 1 << 20) % (room + 1)
    tallies = tallies.at[donor].add(-passed).at[sink].add(passed)
    members = jnp.searchsorted(jnp.cumsum(tallies), jnp.arange(rows * top), side="right").astype(jnp.int32)
    grid = members.reshape(top, rows).T
    grid = grid[jax.random.permutation(jax.random.fold_in(own, 1), rows)]
    offset_by = jax.random.randint(jax.random.fold_in(own, 2), (rows, 1), 0, top)
    return jnp.take_along_axis(grid, (jnp.arange(top)[None, :] + offset_by) % top, axis=1)


def portions_of(number_of, total, limit, lean, full):
    portions = [(1 << 20) // math.isqrt(rank ** lean) + 1 for rank in range(1, number_of + 1)]
    largest = limit if full else min(limit, max(-(-total // number_of), total * portions[0] // sum(portions)))
    least = 1 if total - largest >= number_of - 1 else 0
    holding, spare = [largest] + [least] * (number_of - 1), total - largest - least * (number_of - 1)
    while spare > 0:
        candidates = [i for i in range(1, number_of) if holding[i] < largest] or [i for i in range(1, number_of) if holding[i] < limit]
        pool, left = sum([portions[i] for i in candidates]), spare
        for i in candidates:
            more = min(limit - holding[i], max(1, left * portions[i] // pool), spare)
            holding[i] = holding[i] + more
            spare = spare - more
    return np.array(holding)


def noise(rng, extent, spread, bound, shards=(), kind=jnp.bfloat16):
    result = spread * jax.random.normal(rng, extent, jnp.float32)
    if shards:
        result = result * steps_of(rng, extent, shards, -0.22, 0.18)
    return jnp.clip(result, -bound, bound).astype(kind)


def setup_inputs(seed: int = 0) -> dict:
    keys = jax.random.split(jax.random.key(seed), 21)
    hidden = noise(keys[0], (DRAFT_TOKENS, MODEL_WIDTH), 1.0, 6.0, ((0, 16),))
    attn_gain = jnp.clip(1.0 + 0.18 * jax.random.normal(keys[1], (MODEL_WIDTH,), jnp.float32), 0.1, 1.9)
    attn_router = draw_attn_router(jax.random.fold_in(keys[20], 71), 0)
    attention_expert_pairs = choose_distinct(keys[3], DRAFT_TOKENS, ATTN_EXPERTS, TOPK, 0)
    key_value_weight = noise(keys[4], (2, MODEL_WIDTH, KEY_VALUE_HEADS * HEAD_SIZE), MODEL_WIDTH ** -0.5, 0.125, ((2, 8),))
    query_weight = noise(keys[5], (ATTN_EXPERTS, MODEL_WIDTH, KEY_VALUE_HEADS * HEAD_SIZE), MODEL_WIDTH ** -0.5, 0.125, ((2, 8),))
    output_weight = noise(keys[6], (ATTN_EXPERTS, KEY_VALUE_HEADS * HEAD_SIZE, MODEL_WIDTH), (KEY_VALUE_HEADS * HEAD_SIZE) ** -0.5, 0.125, ((1, 8),))
    paged_key_value_cache = draw_paged_key_value_cache(jax.random.fold_in(keys[20], 71), 0)
    page_table = draw_page_table(jax.random.fold_in(keys[20], 71), 0)
    cache_len = draw_cache_len(jax.random.fold_in(keys[20], 71), 0)
    ancestor = draw_ancestor(jax.random.fold_in(keys[20], 71), 0)
    ffn_gain = jnp.clip(1.0 + 0.18 * jax.random.normal(keys[11], (MODEL_WIDTH,), jnp.float32), 0.1, 1.9)
    ffn_router = draw_ffn_router(jax.random.fold_in(keys[20], 71), 0)
    ffn_route_keys = jax.random.split(jax.random.fold_in(keys[13], 1), DRAFT_TOKENS // ROW_TOK)
    ffn_route_turns = jax.random.permutation(jax.random.fold_in(keys[13], 3), DRAFT_TOKENS // ROW_TOK)
    ffn_route = jax.vmap(lambda own, number: shared_out(jax.random.fold_in(keys[13], 2), own, number, ROW_TOK, FEXP, TOPK, CAP, 1))(ffn_route_keys, ffn_route_turns).reshape((DRAFT_TOKENS, TOPK))
    w_gate_up = noise(keys[14], (FEXP, 2, FF, MODEL_WIDTH), MODEL_WIDTH ** -0.5, 0.125, ((0, 8), (2, 16)))
    w_down = noise(keys[15], (FEXP, FF, MODEL_WIDTH), FF ** -0.5, 0.078125, ((0, 8), (1, 16)))
    accept_path = draw_accept_path(jax.random.fold_in(keys[20], 71), 0)
    accept_count = draw_accept_count(jax.random.fold_in(keys[20], 71), 0)
    mig_slot = draw_mig_slot(jax.random.fold_in(keys[20], 71), 0)
    destination = draw_destination(jax.random.fold_in(keys[20], 71), 0)
    return {"hidden": hidden, "attn_gain": attn_gain, "attn_router": attn_router, "attention_expert_pairs": attention_expert_pairs, "key_value_weight": key_value_weight, "query_weight": query_weight, "output_weight": output_weight, "paged_key_value_cache": paged_key_value_cache, "page_table": page_table, "cache_len": cache_len, "ancestor": ancestor, "ffn_gain": ffn_gain, "ffn_router": ffn_router, "ffn_route": ffn_route, "w_gate_up": w_gate_up, "w_down": w_down, "accept_path": accept_path, "accept_count": accept_count, "mig_slot": mig_slot, "destination": destination}


EPS = 1e-06
NEG = -1e+30

def rms_scale(values, norm_gain):
    mean_sq = lax.optimization_barrier(jnp.mean(values * values, axis=-1, keepdims=True))
    return values * lax.rsqrt(mean_sq + EPS) * norm_gain

def pair_gates(logits, route_ids):
    picked = jnp.take_along_axis(logits, route_ids, axis=1)
    top_value = lax.optimization_barrier(jnp.max(picked, axis=1, keepdims=True))
    exp_terms = jnp.exp(picked - top_value)
    return exp_terms / lax.optimization_barrier(jnp.sum(exp_terms, axis=1, keepdims=True))

def rotate(values, position):
    half_size = values.shape[-1] // 2
    frequency = jnp.exp(jnp.arange(half_size).astype(jnp.float32) * (-2.0 * math.log(10000.0) / values.shape[-1]))
    angles = position.astype(jnp.float32)[:, None] * frequency[None, :]
    table_shape = (values.shape[0],) + (1,) * (values.ndim - 2) + (half_size,)
    cosine = jnp.cos(angles).reshape(table_shape)
    sine_part = jnp.sin(angles).reshape(table_shape)
    first_half = values[..., :half_size]
    second_half = values[..., half_size:]
    return jnp.concatenate([first_half * cosine - second_half * sine_part, second_half * cosine + first_half * sine_part], axis=-1)

def reference(hidden, attn_gain, attn_router, attention_expert_pairs, key_value_weight, query_weight, output_weight, paged_key_value_cache, page_table, cache_len, ancestor, ffn_gain, ffn_router, ffn_route, w_gate_up, w_down, accept_path, accept_count, mig_slot, destination):
    head_column_span = KEY_VALUE_HEADS * HEAD_SIZE
    stream = hidden.astype(jnp.float32)
    normalized_input = rms_scale(stream, attn_gain).astype(jnp.bfloat16)
    logits = jnp.dot(normalized_input.astype(jnp.float32), attn_router, precision=lax.Precision.HIGHEST)
    attn_weights = pair_gates(logits, attention_expert_pairs)
    tree_depth = lax.optimization_barrier(jnp.sum(ancestor, axis=2)) - 1
    position = (cache_len[:, None] + tree_depth).reshape(DRAFT_TOKENS).astype(jnp.int32)
    key_projected = jnp.dot(normalized_input, key_value_weight[0], preferred_element_type=jnp.float32).reshape(DRAFT_TOKENS, KEY_VALUE_HEADS, HEAD_SIZE)
    draft_keys = rotate(key_projected, position).astype(jnp.bfloat16)
    fresh_value_rows = jnp.dot(normalized_input, key_value_weight[1], preferred_element_type=jnp.float32).astype(jnp.bfloat16).reshape(DRAFT_TOKENS, KEY_VALUE_HEADS, HEAD_SIZE)
    query_rows_full = jnp.stack([jnp.dot(normalized_input, query_weight[expert_num], preferred_element_type=jnp.float32) for expert_num in range(ATTN_EXPERTS)], axis=1)
    selected_expert = jnp.take_along_axis(query_rows_full, attention_expert_pairs[:, :, None], axis=1).reshape(DRAFT_TOKENS, 2, KEY_VALUE_HEADS, HEAD_SIZE)
    queries = rotate(selected_expert, position).astype(jnp.bfloat16)
    score_scale = 1.0 / math.sqrt(HEAD_SIZE)

    def one_request(index):
        home_row = index // R_DEV
        page_numbers = home_row * PAGES + page_table[index]
        stored_key_rows = paged_key_value_cache[0][page_numbers].reshape(TABLE_ENTRIES * PAGE_POSITIONS, KEY_VALUE_HEADS, HEAD_SIZE).astype(jnp.float32)
        stored_value_rows = paged_key_value_cache[1][page_numbers].reshape(TABLE_ENTRIES * PAGE_POSITIONS, KEY_VALUE_HEADS, HEAD_SIZE).astype(jnp.float32)
        start_row = (index * DRAFT).astype(jnp.int32)
        own_q = lax.dynamic_slice_in_dim(queries, start_row, DRAFT, 0).astype(jnp.float32)
        own_k = lax.dynamic_slice_in_dim(draft_keys, start_row, DRAFT, 0).astype(jnp.float32)
        own_v = lax.dynamic_slice_in_dim(fresh_value_rows, start_row, DRAFT, 0).astype(jnp.float32)
        tree_mask = lax.dynamic_index_in_dim(ancestor, index, 0, keepdims=False)
        length = cache_len[index]
        valid_c = (jnp.arange(TABLE_ENTRIES * PAGE_POSITIONS, dtype=jnp.int32) < length)[None, None, None, :]
        valid_d = (tree_mask > 0)[:, None, None, :]
        score_c = jnp.einsum('ashd,khd->ashk', own_q, stored_key_rows) * score_scale
        score_d = jnp.einsum('ashd,bhd->ashb', own_q, own_k) * score_scale
        score_c = jnp.where(valid_c, score_c, NEG)
        score_d = jnp.where(valid_d, score_d, NEG)
        top_value = jnp.maximum(lax.optimization_barrier(jnp.max(score_c, axis=-1, keepdims=True)), lax.optimization_barrier(jnp.max(score_d, axis=-1, keepdims=True)))
        exp_c = jnp.where(valid_c, jnp.exp(score_c - top_value), 0.0)
        exp_d = jnp.where(valid_d, jnp.exp(score_d - top_value), 0.0)
        all_terms = lax.optimization_barrier(jnp.sum(exp_c, axis=-1, keepdims=True)) + lax.optimization_barrier(jnp.sum(exp_d, axis=-1, keepdims=True))
        prob_c = lax.optimization_barrier((exp_c / all_terms).astype(jnp.bfloat16)).astype(jnp.float32)
        prob_d = lax.optimization_barrier((exp_d / all_terms).astype(jnp.bfloat16)).astype(jnp.float32)
        return jnp.einsum('ashk,khd->ashd', prob_c, stored_value_rows) + jnp.einsum('ashb,bhd->ashd', prob_d, own_v)
    attended = lax.map(one_request, jnp.arange(REQS, dtype=jnp.int32)).reshape(DRAFT_TOKENS, 2, head_column_span)
    gated_out = attended * attn_weights[:, :, None]
    picked_expert = attention_expert_pairs[:, :, None] == jnp.arange(ATTN_EXPERTS, dtype=jnp.int32)[None, None, :]
    mixed = lax.optimization_barrier(jnp.sum(jnp.where(picked_expert[:, :, :, None], gated_out[:, :, None, :], 0.0), axis=1)).astype(jnp.bfloat16)
    attn_sum = jnp.dot(mixed.reshape(DRAFT_TOKENS, ATTN_EXPERTS * head_column_span), output_weight.reshape(ATTN_EXPERTS * head_column_span, MODEL_WIDTH), preferred_element_type=jnp.float32)
    resid = (stream + attn_sum).astype(jnp.bfloat16)
    normed_ffn = rms_scale(resid.astype(jnp.float32), ffn_gain).astype(jnp.bfloat16)
    ffn_logits = jnp.dot(normed_ffn.astype(jnp.float32), ffn_router, precision=lax.Precision.HIGHEST)
    ffn_weights = pair_gates(ffn_logits, ffn_route)
    member = jnp.any(ffn_route[:, :, None] == jnp.arange(FEXP, dtype=jnp.int32)[None, None, :], axis=1).astype(jnp.int32)
    member_rows = member.reshape(N_REQ, ROW_TOK, FEXP)
    slot_rank = (jnp.cumsum(member_rows, axis=1) - member_rows).reshape(DRAFT_TOKENS, FEXP)
    token_ids = jnp.arange(DRAFT_TOKENS, dtype=jnp.int32)
    token_row = token_ids // ROW_TOK

    def one_expert(expert_num):
        is_member = jnp.take(member, expert_num, axis=1)
        rank_here = jnp.take(slot_rank, expert_num, axis=1)
        target = jnp.where(is_member > 0, token_row * CAP + rank_here, N_REQ * CAP)
        slot_table = jnp.zeros((N_REQ * CAP,), jnp.int32).at[target].set(token_ids, mode='drop')
        gathered = normed_ffn[slot_table]
        weights_here = w_gate_up[expert_num]
        gate_proj = jnp.dot(gathered, weights_here[0].T, preferred_element_type=jnp.float32)
        up_proj = jnp.dot(gathered, weights_here[1].T, preferred_element_type=jnp.float32)
        hidden_units = (jax.nn.silu(gate_proj) * up_proj).astype(jnp.bfloat16)
        return jnp.dot(hidden_units, w_down[expert_num], preferred_element_type=jnp.float32).astype(jnp.bfloat16)
    expert_out = lax.map(one_expert, jnp.arange(FEXP, dtype=jnp.int32))
    slot_of = token_row[:, None] * CAP + jnp.take_along_axis(slot_rank, ffn_route, axis=1)
    picked = expert_out[ffn_route, slot_of].astype(jnp.float32)
    ffn_sum = lax.optimization_barrier(jnp.sum(ffn_weights[:, :, None] * picked, axis=1))
    layer_out = (resid.astype(jnp.float32) + ffn_sum).astype(jnp.bfloat16)
    flat_pool = paged_key_value_cache.reshape(2, TOTAL_PAGES * PAGE_POSITIONS, head_column_span)
    req_ids = jnp.arange(REQS, dtype=jnp.int32)
    step_ids = jnp.arange(ACC, dtype=jnp.int32)
    places = cache_len[:, None] + step_ids[None, :]
    page_slot = jnp.take_along_axis(page_table, places // PAGE_POSITIONS, axis=1)
    flat_index = ((req_ids // R_DEV)[:, None] * PAGES + page_slot) * PAGE_POSITIONS + places % PAGE_POSITIONS
    flat_index = jnp.where(step_ids[None, :] < accept_count[:, None], flat_index, TOTAL_PAGES * PAGE_POSITIONS)
    source = (req_ids[:, None] * DRAFT + accept_path).reshape(-1)
    fresh_rows = jnp.stack([draft_keys.reshape(DRAFT_TOKENS, head_column_span)[source], fresh_value_rows.reshape(DRAFT_TOKENS, head_column_span)[source]])
    flat_pool = flat_pool.at[:, flat_index.reshape(-1)].set(fresh_rows, mode='drop')
    new_pool = flat_pool.reshape(2, TOTAL_PAGES, PAGE_POSITIONS, head_column_span)
    row_ids = jnp.arange(N_REQ, dtype=jnp.int32)
    moving_req = row_ids * R_DEV + mig_slot
    src_pages = (row_ids[:, None] * PAGES + page_table[moving_req, :MIGP]).reshape(-1)
    dst_pages = (destination[:, None] * PAGES + PAGES - MIGP + jnp.arange(MIGP, dtype=jnp.int32)[None, :]).reshape(-1)
    new_pool = new_pool.at[:, dst_pages].set(new_pool[:, src_pages])
    return (layer_out, new_pool)
```

```python
import math

import jax
import jax.numpy as jnp
from jax import lax
from jax.experimental import pallas as pl
from jax.experimental.pallas import tpu as pltpu
from jax.sharding import PartitionSpec as P

EPS = 1e-06
NEG = -1e30
BF16 = jnp.bfloat16
F32 = jnp.float32
MESH = pl.DeviceIdType.MESH
ENTRIES = 30
CAP = 96
QUARTER = 512
HALF = 1024


def dot_nn(a, b):
    return lax.dot_general(a, b, (((1,), (0,)), ((), ())), preferred_element_type=F32)


def dot_nt(a, b):
    return lax.dot_general(a, b, (((1,), (1,)), ((), ())), preferred_element_type=F32)


def iota(shape, axis):
    return lax.broadcasted_iota(jnp.int32, shape, axis)


def split_dot(rows, weights):
    high = weights.astype(BF16)
    rest = weights - high.astype(F32)
    middle = rest.astype(BF16)
    low = (rest - middle.astype(F32)).astype(BF16)
    return dot_nt(rows, high) + dot_nt(rows, middle) + dot_nt(rows, low)


def as_columns(rows):
    n = rows.shape[1]
    eye = (iota((n, n), 0) == iota((n, n), 1)).astype(F32).astype(BF16)
    return dot_nt(eye, rows.astype(F32).astype(BF16))


def pair_gates(logits, columns):
    lanes = iota(logits.shape, 1).astype(F32)
    picked = [
        jnp.sum(jnp.where(lanes == columns[:, s : s + 1], logits, 0.0), axis=1, keepdims=True)
        for s in range(2)
    ]
    top = jnp.maximum(picked[0], picked[1])
    terms = [jnp.exp(value - top) for value in picked]
    total = terms[0] + terms[1]
    return [term / total for term in terms]


def attend_kernel(
    len_s,
    table_s,
    count_s,
    mig_s,
    hidden_r,
    gain_r,
    router_r,
    pairs_r,
    anc_r,
    path_r,
    route_r,
    kvw_h,
    qw_h,
    ow_h,
    pool_h,
    part_r,
    mover_r,
    disp_r,
    dispt_r,
    out_h,
    wbuf,
    owbuf,
    pool,
    norm_v,
    cos_v,
    sin_v,
    qsel,
    q_v,
    kd,
    vd,
    scores,
    peak,
    acc,
    mix,
    ent_page,
    ent_req,
    ent_cnt,
    sems,
):
    loads = []
    for c in range(2):
        loads.append(pltpu.make_async_copy(kvw_h.at[c], wbuf.at[c], sems.at[c]))
    for c in range(4):
        loads.append(pltpu.make_async_copy(qw_h.at[c], wbuf.at[2 + c], sems.at[2 + c]))
    for c in range(2):
        loads.append(pltpu.make_async_copy(pool_h.at[c], pool.at[c], sems.at[6 + c]))
    loads.append(pltpu.make_async_copy(ow_h, owbuf, sems.at[8]))
    for load in loads:
        load.start()

    offset = jnp.int32(0)
    for i in range(4):
        length = len_s[i]
        pages = (length + (16 + 127)) // 128

        def add_entry(j, carry, i=i, length=length, offset=offset):
            e = offset + j
            ent_page[e] = table_s[i, j]
            ent_req[e] = jnp.int32(i)
            ent_cnt[e] = jnp.clip(length - j * 128, 0, 128)
            return carry

        lax.fori_loop(0, pages, add_entry, 0)
        offset = offset + pages

    gain = gain_r[...]

    def norm_rows(j, carry):
        rows = pl.ds(pl.multiple_of(j * 32, 32), 32)
        x = hidden_r[rows, :].astype(F32)
        mean_sq = jnp.mean(x * x, axis=1, keepdims=True)
        norm_v[rows, :] = (x * lax.rsqrt(mean_sq + EPS) * gain).astype(BF16)
        return carry

    lax.fori_loop(0, 8, norm_rows, 0)

    lane = iota((64, 128), 1)
    entry = jnp.where(lane >= 64, lane - 64, lane).astype(F32)
    frequency = jnp.exp(entry * (-2.0 * math.log(10000.0) / 128))
    for i in range(4):
        depth = jnp.sum(anc_r[i].astype(F32), axis=1, keepdims=True) - 1.0
        angles = (depth + len_s[i].astype(F32)) * frequency
        cos_v[i * 64 : (i + 1) * 64, :] = jnp.cos(angles)
        sine = jnp.sin(angles)
        sin_v[i * 64 : (i + 1) * 64, :] = jnp.where(lane < 64, -sine, sine)

    def rotate(values, i):
        rows = slice(i * 64, (i + 1) * 64)
        return values * cos_v[rows, :] + pltpu.roll(values, 64, 1) * sin_v[rows, :]

    pair_cols = as_columns(pairs_r[...])
    gates = pair_gates(split_dot(norm_v[...], router_r[...]), pair_cols)

    zeros = jnp.zeros((64, 256), BF16)
    loads[0].wait()
    proj = dot_nn(norm_v[...], wbuf[0])
    for i in range(4):
        for h in range(2):
            cols = slice(h * 128, (h + 1) * 128)
            kd[i, 0:64, cols] = rotate(proj[i * 64 : (i + 1) * 64, cols], i).astype(BF16)
        kd[i, 64:128, :] = zeros
    loads[1].wait()
    proj = dot_nn(norm_v[...], wbuf[1])
    for i in range(4):
        vd[i, 0:64, :] = proj[i * 64 : (i + 1) * 64, :].astype(BF16)
        vd[i, 64:128, :] = zeros

    for e in range(4):
        loads[2 + e].wait()
        proj = dot_nn(norm_v[...], wbuf[2 + e])
        for s in range(2):
            if e == 0:
                qsel[s] = proj
            else:
                qsel[s] = jnp.where(pair_cols[:, s : s + 1] == float(e), proj, qsel[s])
    for i in range(4):
        for s in range(2):
            for h in range(2):
                picked = qsel[s, i * 64 : (i + 1) * 64, h * 128 : (h + 1) * 128]
                q_v[h, i, s * 64 : (s + 1) * 64, :] = rotate(picked, i).astype(BF16)

    scale = 1.0 / math.sqrt(128)
    wide = iota((128, 128), 1)
    for i in range(4):
        tree = anc_r[i].astype(F32)
        for h in range(2):
            cols = slice(h * 128, (h + 1) * 128)
            score = dot_nt(q_v[h, i], kd[i, 0:64, cols]) * scale
            for s in range(2):
                rows = slice(s * 64, (s + 1) * 64)
                masked = jnp.where(tree > 0.0, score[rows, :], NEG)
                scores[h, ENTRIES + i, rows, 0:64] = masked
                peak[h, i, rows, 0:64] = masked
            scores[h, ENTRIES + i, :, 64:128] = jnp.full((128, 64), NEG, F32)
            peak[h, i, :, 64:128] = jnp.full((128, 64), NEG, F32)
    loads[6].wait()

    def score_entries(step, carry):
        for k in range(5):
            e = step * 5 + k
            page, i, count = ent_page[e], ent_req[e], ent_cnt[e]
            keys = pool[0, page]
            for h in range(2):
                score = dot_nt(q_v[h, i], keys[:, h * 128 : (h + 1) * 128]) * scale
                score = jnp.where(wide < count, score, NEG)
                scores[h, e] = score
                peak[h, i] = jnp.maximum(peak[h, i], score)
        return carry

    lax.fori_loop(0, ENTRIES // 5, score_entries, 0)

    ones = jnp.ones((128, 128), BF16)
    loads[7].wait()
    for i in range(4):
        for h in range(2):
            top = jnp.broadcast_to(jnp.max(peak[h, i], axis=1, keepdims=True), (128, 128))
            peak[h, i] = top
            terms = jnp.exp(scores[h, ENTRIES + i] - top).astype(BF16)
            values = jnp.concatenate([vd[i, :, h * 128 : (h + 1) * 128], ones], axis=1)
            acc[h, i] = dot_nn(terms, values)

    def sum_entries(step, carry):
        for k in range(5):
            e = step * 5 + k
            page, i = ent_page[e], ent_req[e]
            page_values = pool[1, page]
            for h in range(2):
                terms = jnp.exp(scores[h, e] - peak[h, i]).astype(BF16)
                values = jnp.concatenate([page_values[:, h * 128 : (h + 1) * 128], ones], axis=1)
                acc[h, i] += dot_nn(terms, values)
        return carry

    lax.fori_loop(0, ENTRIES // 5, sum_entries, 0)

    place = iota((128, 16), 0)
    step_ids = iota((128, 16), 1)
    tokens = iota((128, 64), 1).astype(F32)
    for i in range(4):
        length, count = len_s[i], count_s[i]
        first = length // 128
        path = path_r[i : i + 1, :].astype(F32)
        for extra in range(2):
            spot = first + extra
            page = table_s[i, jnp.minimum(spot, ENTRIES - 1)]
            hit = (place + (spot * 128 - length) == step_ids) & (step_ids < count)
            taken = jnp.sum(jnp.where(hit, 1.0, 0.0), axis=1, keepdims=True)
            token = jnp.sum(jnp.where(hit, path, 0.0), axis=1, keepdims=True)
            token = jnp.where(taken > 0.0, token, -1.0)
            choose = jnp.where(tokens == token, 1.0, 0.0).astype(BF16)
            for which, fresh in ((0, kd), (1, vd)):
                new = dot_nn(choose, fresh[i, 0:64, :])
                old = pool[which, page].astype(F32)
                pool[which, page] = jnp.where(taken > 0.0, new, old).astype(BF16)
    moving = mig_s[0]
    for which in range(2):
        for j in range(2):
            mover_r[which, j] = pool[which, table_s[moving, j]]
    stores = [
        pltpu.make_async_copy(
            pool.at[which, pl.ds(0, ENTRIES)], out_h.at[which, pl.ds(0, ENTRIES)], sems.at[9 + which]
        )
        for which in range(2)
    ]
    for store in stores:
        store.start()

    for i in range(4):
        rows = slice(i * 64, (i + 1) * 64)
        for h in range(2):
            total = acc[h, i]
            attended = total[:, 0:128] / total[:, 128:256]
            gated = [attended[s * 64 : (s + 1) * 64, :] * gates[s][rows, :] for s in range(2)]
            for e in range(4):
                mixed = jnp.where(pair_cols[rows, 0:1] == float(e), gated[0], 0.0) + jnp.where(
                    pair_cols[rows, 1:2] == float(e), gated[1], 0.0
                )
                mix[rows, e * 256 + h * 128 : e * 256 + (h + 1) * 128] = mixed.astype(BF16)

    expert = lax.axis_index("head")
    route = route_r[...]
    named = jnp.where(route == expert, 1.0, 0.0)
    member = named[0:1, :] + named[1:2, :]
    before = (iota((256, 256), 0) < iota((256, 256), 1)).astype(F32).astype(BF16)
    rank = dot_nn(jnp.broadcast_to(member, (8, 256)).astype(BF16), before)[0:1, :]
    slots = iota((CAP, 256), 0).astype(F32)
    chosen = jnp.where(slots == rank, 1.0, 0.0) * member
    disp_r[...] = chosen.astype(BF16)
    eye = (iota((256, 256), 0) == iota((256, 256), 1)).astype(F32).astype(BF16)
    dispt_r[...] = dot_nt(eye, chosen.astype(BF16)).astype(BF16)

    loads[8].wait()
    for n in range(4):
        cols = slice(n * QUARTER, (n + 1) * QUARTER)
        out = dot_nn(mix[:, 0:256], owbuf[0, :, cols])
        for e in range(1, 4):
            out = out + dot_nn(mix[:, e * 256 : (e + 1) * 256], owbuf[e, :, cols])
        for b in range(8):
            part_r[b % 2, b // 2, :, cols] = out[b * 32 : (b + 1) * 32, :].astype(BF16)
    for store in stores:
        store.wait()


def attend(args):
    vmem = pl.BlockSpec(memory_space=pltpu.VMEM)
    smem = pl.BlockSpec(memory_space=pltpu.SMEM)
    anywhere = pl.BlockSpec(memory_space=pl.ANY)
    return pl.pallas_call(
        attend_kernel,
        out_shape=(
            jax.ShapeDtypeStruct((2, 4, 32, 2048), BF16),
            jax.ShapeDtypeStruct((2, 2, 128, 256), BF16),
            jax.ShapeDtypeStruct((CAP, 256), BF16),
            jax.ShapeDtypeStruct((256, CAP), BF16),
            jax.ShapeDtypeStruct((2, 32, 128, 256), BF16),
        ),
        in_specs=[smem] * 4 + [vmem] * 7 + [anywhere] * 4,
        out_specs=(vmem, vmem, vmem, vmem, anywhere),
        scratch_shapes=[
            pltpu.VMEM((6, 2048, 256), BF16),
            pltpu.VMEM((4, 256, 2048), BF16),
            pltpu.VMEM((2, 32, 128, 256), BF16),
            pltpu.VMEM((256, 2048), BF16),
            pltpu.VMEM((256, 128), F32),
            pltpu.VMEM((256, 128), F32),
            pltpu.VMEM((2, 256, 256), F32),
            pltpu.VMEM((2, 4, 128, 128), BF16),
            pltpu.VMEM((4, 128, 256), BF16),
            pltpu.VMEM((4, 128, 256), BF16),
            pltpu.VMEM((2, ENTRIES + 4, 128, 128), F32),
            pltpu.VMEM((2, 4, 128, 128), F32),
            pltpu.VMEM((2, 4, 128, 256), F32),
            pltpu.VMEM((256, 1024), BF16),
            pltpu.SMEM((32,), jnp.int32),
            pltpu.SMEM((32,), jnp.int32),
            pltpu.SMEM((32,), jnp.int32),
            pltpu.SemaphoreType.DMA((11,)),
        ],
        name="attend",
    )(*args)


def greet(devices):
    barrier = pltpu.get_barrier_semaphore()
    for device in devices:
        pl.semaphore_signal(barrier, inc=1, device_id=device, device_id_type=MESH)
    pl.semaphore_wait(barrier, len(devices))


class Sender:
    def __init__(self, send_sems, recv_sems):
        self.send_sems, self.recv_sems = send_sems, recv_sems
        self.copies = {}

    def send(self, index, src, dst, device):
        copy = pltpu.make_async_remote_copy(
            src_ref=src,
            dst_ref=dst,
            send_sem=self.send_sems.at[index],
            recv_sem=self.recv_sems.at[index],
            device_id=device,
            device_id_type=MESH,
        )
        copy.start()
        self.copies[index] = copy

    def arrived(self, index):
        self.copies[index].wait_recv()

    def drain(self):
        for copy in self.copies.values():
            copy.wait_send()


def head_place():
    h = lax.axis_index("head")
    z, core = h // 2, lax.rem(h, 2)

    def along(step):
        return {"head": lax.rem(z + (step + 4), 4) * 2 + core}

    return h, z, core, along, {"head": z * 2 + (1 - core)}


def reduce_over_head(own, got, relay, near, far, sent, sender, base):
    h, z, core, along, partner = head_place()
    order = (2, 1, 3, 0)
    for k, step in enumerate(order):
        zz = lax.rem(z + step, 4)
        sender.send(base + k, own.at[1 - core, zz], got.at[zz], partner)

    def columns(q):
        return pl.ds(q * HALF, HALF)

    for k, step in enumerate(order):
        zz = lax.rem(z + step, 4)
        sender.arrived(base + k)
        sent[step] = (own[core, zz].astype(F32) + got[zz].astype(F32)).astype(BF16)
        if step == 2:
            for q, s in ((0, 1), (1, -1)):
                sender.send(base + 4 + q, sent.at[2, :, columns(q)], relay.at[q], along(s))
        if step == 1:
            sender.send(base + 6 + 1, sent.at[1, :, columns(1)], near.at[1], along(1))
        if step == 3:
            sender.send(base + 6, sent.at[3, :, columns(0)], near.at[0], along(-1))
    for q, s in ((0, 1), (1, -1)):
        sender.arrived(base + 4 + q)
        passed = relay[q].astype(F32) + sent[s % 4, :, columns(q)].astype(F32)
        sent[s % 4, :, columns(q)] = passed.astype(BF16)
        sender.send(base + 8 + q, sent.at[s % 4, :, columns(q)], far.at[q], along(s))
    halves = []
    for q in range(2):
        sender.arrived(base + 6 + q)
        sender.arrived(base + 8 + q)
        halves.append(
            sent[0, :, columns(q)].astype(F32) + near[q].astype(F32) + far[q].astype(F32)
        )
    return halves


HEAD_SCRATCH = [
    pltpu.VMEM((4, 32, 2048), BF16),
    pltpu.VMEM((2, 32, HALF), BF16),
    pltpu.VMEM((2, 32, HALF), BF16),
    pltpu.VMEM((2, 32, HALF), BF16),
    pltpu.VMEM((4, 32, 2048), BF16),
]


def head_kernel(
    dest_s,
    part_r,
    hidden_r,
    gain_r,
    router_r,
    route_r,
    mover_r,
    disp_r,
    outb_r,
    resid_r,
    gate_r,
    incoming_r,
    got,
    relay,
    near,
    far,
    sent,
    norms,
    mb,
    sb,
    mr,
    send_sems,
    recv_sems,
):
    h, z, core, along, partner = head_place()
    r = lax.axis_index("req")
    x, y = r // 4, lax.rem(r, 4)

    def place(which, u, v):
        return u * 4 + v if which == 0 else v * 4 + u

    def shift(u, step):
        return lax.rem(u + (step + 4), 4)

    spots = ((x, y), (y, x))
    devices = [partner, along(1), along(-1)]
    for which, (u, v) in enumerate(spots):
        devices += [{"req": place(which, shift(u, d), v)} for d in (1, 2, 3)]
    greet(devices)
    sender = Sender(send_sems, recv_sems)

    for which, (u, v) in enumerate(spots):
        for d in (1, 2, 3):
            sender.send(
                24 + which * 3 + d - 1,
                mover_r.at[which],
                mb.at[which, d],
                {"req": place(which, shift(u, d), v)},
            )
        mb[which, 0] = mover_r[which]

    halves = reduce_over_head(part_r, got, relay, near, far, sent, sender, 0)

    rows = pl.ds(pl.multiple_of(h * 32, 32), 32)
    sums = []
    for q in range(2):
        cols = slice(q * HALF, (q + 1) * HALF)
        resid = (hidden_r[rows, cols].astype(F32) + halves[q]).astype(BF16)
        resid_r[:, cols] = resid
        wide = resid.astype(F32)
        sums.append(jnp.sum(wide * wide, axis=1, keepdims=True))
    scale = lax.rsqrt((sums[0] + sums[1]) * (1.0 / 2048) + EPS)
    for q in range(2):
        cols = slice(q * HALF, (q + 1) * HALF)
        norms[h, :, cols] = (resid_r[:, cols].astype(F32) * scale * gain_r[:, cols]).astype(BF16)

    def block(step, q):
        return norms.at[shift(z, step) * 2 + core, :, pl.ds(q * HALF, HALF)]

    turns = ((0, 1), (1, -1))
    for q, s in turns:
        sender.send(10 + q, block(0, q), block(0, q), along(s))
    for q, s in turns:
        sender.send(12 + q, block(0, q), block(0, q), along(-s))
    for q, s in turns:
        sender.send(16 + q, block(0, q), block(0, q), partner)

    for k in range(24, 30):
        sender.arrived(k)
    for which, (u, v) in enumerate(spots):
        for d in (0, 1, 2, 3):
            target = place(which, u, shift(v, d))
            pick = jnp.int32(0)
            for k in (1, 2, 3):
                found = dest_s[place(which, shift(u, -k), v)] == target
                pick = jnp.where(found, jnp.int32(k), pick)
            if d == 0:
                mr[which, 0] = mb[which, pick]
            else:
                sb[which, d - 1] = mb[which, pick]
                sender.send(
                    30 + which * 3 + d - 1, sb.at[which, d - 1], mr.at[which, d], {"req": target}
                )

    for q, s in turns:
        sender.arrived(10 + q)
        sender.send(14 + q, block(-s, q), block(-s, q), along(s))
        sender.send(18 + q, block(-s, q), block(-s, q), partner)
    for q, s in turns:
        sender.arrived(12 + q)
        sender.send(20 + q, block(s, q), block(s, q), partner)
    for q, s in turns:
        sender.arrived(14 + q)
        sender.send(22 + q, block(2, q), block(2, q), partner)
    for k in range(16, 24):
        sender.arrived(k)

    for which in range(2):
        for d in (1, 2, 3):
            sender.arrived(30 + which * 3 + d - 1)
    for which, (u, v) in enumerate(spots):
        back = jnp.int32(0)
        for d in (1, 2, 3):
            for k in range(4):
                found = dest_s[place(which, shift(u, k), shift(v, -d))] == r
                back = jnp.where(found, jnp.int32(d), back)
        incoming_r[which] = mr[which, back]

    normed = norms[...].reshape(256, 2048)
    for q in range(4):
        outb_r[q] = dot_nn(disp_r[...], normed[:, q * QUARTER : (q + 1) * QUARTER]).astype(BF16)
    route_cols = as_columns(route_r[...])
    weights = pair_gates(split_dot(normed, router_r[...]), route_cols)
    expert = h.astype(F32)
    mine = jnp.where(route_cols[:, 0:1] == expert, weights[0], 0.0) + jnp.where(
        route_cols[:, 1:2] == expert, weights[1], 0.0
    )
    gate_r[...] = jnp.broadcast_to(mine, (256, 128))
    sender.drain()


def head_stage(args):
    vmem = pl.BlockSpec(memory_space=pltpu.VMEM)
    smem = pl.BlockSpec(memory_space=pltpu.SMEM)
    return pl.pallas_call(
        head_kernel,
        out_shape=(
            jax.ShapeDtypeStruct((4, CAP, QUARTER), BF16),
            jax.ShapeDtypeStruct((32, 2048), BF16),
            jax.ShapeDtypeStruct((256, 128), F32),
            jax.ShapeDtypeStruct((2, 2, 128, 256), BF16),
        ),
        in_specs=[smem] + [vmem] * 7,
        out_specs=(vmem, vmem, vmem, vmem),
        scratch_shapes=HEAD_SCRATCH
        + [
            pltpu.VMEM((8, 32, 2048), BF16),
            pltpu.VMEM((2, 4, 2, 128, 256), BF16),
            pltpu.VMEM((2, 3, 2, 128, 256), BF16),
            pltpu.VMEM((2, 4, 2, 128, 256), BF16),
            pltpu.SemaphoreType.DMA((36,)),
            pltpu.SemaphoreType.DMA((36,)),
        ],
        compiler_params=pltpu.CompilerParams(collective_id=1, has_side_effects=True),
        name="head_stage",
    )(*args)


TURNS = ((0, 1), (0, -1), (1, 1), (1, -1))
LAST = 60


def ffn_kernel(
    outb_r,
    resid_r,
    gate_r,
    dispt_r,
    wgu_h,
    wd_h,
    layer_r,
    rows_v,
    parts,
    ra,
    rb,
    rc,
    rd,
    re,
    rf,
    wgu,
    wd,
    eo,
    blocks,
    got,
    relay,
    near,
    far,
    sent,
    load_sems,
    send_sems,
    recv_sems,
    back_send,
    back_recv,
    head_send,
    head_recv,
):
    h, z, core, along, partner = head_place()
    r = lax.axis_index("req")
    x, y = r // 4, lax.rem(r, 4)

    def shift(u, step):
        return lax.rem(u + (step + 4), 4)

    def spot(q):
        return (x, y) if TURNS[q][0] == 0 else (y, x)

    def at(q, du, dv):
        u, v = spot(q)
        u, v = shift(u, du), shift(v, dv)
        return u * 4 + v if TURNS[q][0] == 0 else v * 4 + u

    loads = [
        pltpu.make_async_copy(wgu_h, wgu, load_sems.at[0]),
        pltpu.make_async_copy(wd_h, wd, load_sems.at[1]),
    ]
    for load in loads:
        load.start()
    greet(
        [{"req": at(0, d, 0)} for d in (1, -1)]
        + [{"req": at(0, 0, d)} for d in (1, -1)]
        + [partner, along(1), along(-1)]
    )

    sender = Sender(send_sems, recv_sems)

    def pass_on(q, message, du, dv, step_u, step_v):
        here = rows_v.at[q, at(q, du, dv)]
        sender.send(q * 15 + message, here, here, {"req": at(q, step_u, step_v)})

    for q in range(4):
        rows_v[q, r] = outb_r[q]
    for q, (_, s) in enumerate(TURNS):
        pass_on(q, 0, 0, 0, s, 0)
        pass_on(q, 1, 0, 0, -s, 0)
    for q, (_, s) in enumerate(TURNS):
        pass_on(q, 3, 0, 0, 0, s)
        pass_on(q, 4, 0, 0, 0, -s)

    def offset(k, s):
        return (0, -s, s, 2)[k]

    def spread(q, k, s):
        pass_on(q, 3 + 3 * k, offset(k, s), 0, 0, s)
        pass_on(q, 4 + 3 * k, offset(k, s), 0, 0, -s)

    def forward(q, k, s):
        sender.arrived(q * 15 + 3 + 3 * k)
        pass_on(q, 5 + 3 * k, offset(k, s), -s, 0, s)

    for q, (_, s) in enumerate(TURNS):
        sender.arrived(q * 15)
        pass_on(q, 2, -s, 0, s, 0)
        spread(q, 1, s)
    for q, (_, s) in enumerate(TURNS):
        sender.arrived(q * 15 + 1)
        spread(q, 2, s)
    for q, (_, s) in enumerate(TURNS):
        forward(q, 0, s)
    for q, (_, s) in enumerate(TURNS):
        sender.arrived(q * 15 + 2)
        spread(q, 3, s)
    for k in (1, 2, 3):
        for q, (_, s) in enumerate(TURNS):
            forward(q, k, s)
    for k in range(4):
        for q in range(4):
            sender.arrived(q * 15 + 4 + 3 * k)
            sender.arrived(q * 15 + 5 + 3 * k)

    for load in loads:
        load.wait()

    def some_rows(j, carry):
        group = pl.ds(j * 4, 4)
        gate = jnp.zeros((4 * CAP, 352), F32)
        up = jnp.zeros((4 * CAP, 352), F32)
        for q in range(4):
            held = rows_v[q, group].reshape(4 * CAP, QUARTER)
            cols = slice(q * QUARTER, (q + 1) * QUARTER)
            gate = gate + dot_nt(held, wgu[0, :, cols])
            up = up + dot_nt(held, wgu[1, :, cols])
        units = (jax.nn.silu(gate) * up).astype(BF16)
        for q in range(4):
            out = dot_nn(units, wd[:, q * QUARTER : (q + 1) * QUARTER])
            parts[q, group] = out.astype(BF16).reshape(4, CAP, QUARTER)
        return carry

    lax.fori_loop(0, 4, some_rows, 0)

    back = Sender(back_send, back_recv)

    def add(q, du, dv, *others):
        block = at(q, du, dv)
        total = parts[q, block].astype(F32)
        for other in others:
            total = total + other.astype(F32)
        parts[q, block] = total.astype(BF16)

    def turn_order(s):
        return (2, (-s) % 4, s % 4, 0)

    for place in range(4):
        for q, (_, s) in enumerate(TURNS):
            di = turn_order(s)[place]
            back.send(
                q * 15 + di, parts.at[q, at(q, di, 2)], ra.at[q, di], {"req": at(q, 0, s)}
            )
            back.send(
                q * 15 + 4 + di, parts.at[q, at(q, di, -s)], rb.at[q, di], {"req": at(q, 0, -s)}
            )
    for place in range(4):
        for q, (_, s) in enumerate(TURNS):
            di = turn_order(s)[place]
            back.arrived(q * 15 + di)
            add(q, di, s, ra[q, di])
            back.send(
                q * 15 + 8 + di, parts.at[q, at(q, di, s)], rc.at[q, di], {"req": at(q, 0, s)}
            )
    for place in range(4):
        for q, (_, s) in enumerate(TURNS):
            di = turn_order(s)[place]
            back.arrived(q * 15 + 4 + di)
            back.arrived(q * 15 + 8 + di)
            add(q, di, 0, rb[q, di], rc[q, di])
            if place == 0:
                back.send(q * 15 + 12, parts.at[q, at(q, 2, 0)], rd.at[q], {"req": at(q, s, 0)})
            if place == 1:
                back.send(q * 15 + 13, parts.at[q, at(q, -s, 0)], re.at[q], {"req": at(q, -s, 0)})
    for q, (_, s) in enumerate(TURNS):
        back.arrived(q * 15 + 12)
        add(q, s, 0, rd[q])
        back.send(q * 15 + 14, parts.at[q, at(q, s, 0)], rf.at[q], {"req": at(q, s, 0)})
    for q in range(4):
        back.arrived(q * 15 + 13)
        back.arrived(q * 15 + 14)
        total = parts[q, r].astype(F32) + re[q].astype(F32) + rf[q].astype(F32)
        eo[q] = total.astype(BF16)

    weight = gate_r[:, 0:1]
    for q in range(4):
        cols = slice(q * QUARTER, (q + 1) * QUARTER)
        out = dot_nn(dispt_r[...], eo[q]) * weight
        for b in range(8):
            blocks[b % 2, b // 2, :, cols] = out[b * 32 : (b + 1) * 32, :].astype(BF16)
    last = Sender(head_send, head_recv)
    halves = reduce_over_head(blocks, got, relay, near, far, sent, last, 0)
    for q in range(2):
        cols = slice(q * HALF, (q + 1) * HALF)
        layer_r[:, cols] = (resid_r[:, cols].astype(F32) + halves[q]).astype(BF16)
    sender.drain()
    back.drain()
    last.drain()


def ffn_stage(args):
    vmem = pl.BlockSpec(memory_space=pltpu.VMEM)
    anywhere = pl.BlockSpec(memory_space=pl.ANY)
    block = (CAP, QUARTER)
    return pl.pallas_call(
        ffn_kernel,
        out_shape=jax.ShapeDtypeStruct((32, 2048), BF16),
        in_specs=[vmem] * 4 + [anywhere] * 2,
        out_specs=vmem,
        scratch_shapes=[
            pltpu.VMEM((4, 16) + block, BF16),
            pltpu.VMEM((4, 16) + block, BF16),
            pltpu.VMEM((4, 4) + block, BF16),
            pltpu.VMEM((4, 4) + block, BF16),
            pltpu.VMEM((4, 4) + block, BF16),
            pltpu.VMEM((4,) + block, BF16),
            pltpu.VMEM((4,) + block, BF16),
            pltpu.VMEM((4,) + block, BF16),
            pltpu.VMEM((2, 352, 2048), BF16),
            pltpu.VMEM((352, 2048), BF16),
            pltpu.VMEM((4,) + block, BF16),
            pltpu.VMEM((2, 4, 32, 2048), BF16),
        ]
        + HEAD_SCRATCH
        + [
            pltpu.SemaphoreType.DMA((2,)),
            pltpu.SemaphoreType.DMA((LAST,)),
            pltpu.SemaphoreType.DMA((LAST,)),
            pltpu.SemaphoreType.DMA((LAST,)),
            pltpu.SemaphoreType.DMA((LAST,)),
            pltpu.SemaphoreType.DMA((10,)),
            pltpu.SemaphoreType.DMA((10,)),
        ],
        compiler_params=pltpu.CompilerParams(collective_id=2, has_side_effects=True),
        name="ffn_stage",
    )(*args)


def on_device(
    hidden,
    attn_gain,
    attn_router,
    attention_expert_pairs,
    key_value_weight,
    query_weight,
    output_weight,
    paged_key_value_cache,
    page_table,
    cache_len,
    ancestor,
    ffn_gain,
    ffn_router,
    ffn_route,
    w_gate_up,
    w_down,
    accept_path,
    accept_count,
    mig_slot,
    destination,
):
    route = ffn_route.T
    part, mover, disp, dispt, pool = attend(
        (
            cache_len,
            page_table,
            accept_count,
            mig_slot,
            hidden,
            attn_gain.reshape(1, -1),
            attn_router.T,
            attention_expert_pairs.T,
            ancestor,
            accept_path,
            route,
            key_value_weight,
            query_weight,
            output_weight,
            paged_key_value_cache,
        )
    )
    outb, resid, gate, incoming = head_stage(
        (
            destination,
            part,
            hidden,
            ffn_gain.reshape(1, -1),
            ffn_router.T,
            route,
            mover,
            disp,
        )
    )
    layer_out = ffn_stage((outb, resid, gate, dispt, w_gate_up[0], w_down[0]))
    pool = lax.dynamic_update_slice(pool, incoming, (0, ENTRIES, 0, 0))
    return (layer_out, pool)


def solution(mesh):
    return jax.shard_map(
        on_device,
        mesh=mesh,
        in_specs=(
            P("req", None),
            P(),
            P(),
            P("req", None),
            P(None, None, "head"),
            P(None, None, "head"),
            P(None, "head", None),
            P(None, "req", None, "head"),
            P("req", None),
            P("req"),
            P("req", None, None),
            P(),
            P(),
            P("req", None),
            P("head", None, "req", None),
            P("head", "req", None),
            P("req", None),
            P("req"),
            P("req"),
            P(),
        ),
        out_specs=(P(("req", "head"), None), P(None, "req", None, "head")),
        check_vma=False,
    )
```
